128 devices in a mesh: row: 16 (over y_lo, x, core), col: 8 (over z, y_hi).
Axes of the slice: x: 4, y: 4 (y_hi: 2, y_lo: 2; y = y_hi * 2 + y_lo), z: 4, core: 2. Of those that a mesh axis runs over, the one named last changes fastest.
Arguments:
- grad_out: bfloat16 [2048, 16384], P('col', 'row'), may hold values from -6 to 6
- gate_act: bfloat16 [2048, 26624], P('row', 'col'), may hold values from -8 to 8
- up_act: bfloat16 [2048, 26624], P('row', 'col'), may hold values from -6 to 6
- down_weight: bfloat16 [26624, 16384], P('col', 'row'), may hold values from -0.046875 to 0.046875
Outputs:
- grad_gate: bfloat16 [2048, 26624], P('row', 'col')
- grad_up: bfloat16 [2048, 26624], P('row', 'col')
- grad_down: bfloat16 [26624, 16384], P('col', 'row')
The draws below stay inside these ranges and needn't reach their ends.
All inputs are finite; a program needn't handle non-finite values.
Results may differ from the reference program's by a relative error of at most 0.0049.
Values may be sent and summed in bfloat16 or wider, within the bound.
A program may use at most 448 MiB of HBM per device.

```python
import jax
import jax.numpy as jnp
from jax import lax

D = 16384
F = 26624
TOKENS = 2048


def strengthened(array, rng, source, target, shards_of, factor):
    def block_of(position):
        return (jnp.arange(array.shape[position]) // (array.shape[position] // shards_of)).reshape((-1,) + (1,) * (array.ndim - 1 - position))

    one_side = jax.random.permutation(rng, shards_of)[block_of(target)]
    other_side = (block_of(target) + shards_of // 2) % shards_of
    return jnp.where((block_of(source) == one_side) | (block_of(source) == other_side), factor * array, array)


def block_scale(rng, shape, pieces, least, largest):
    def one(axis_at, parts):
        draws = jax.random.uniform(jax.random.fold_in(jax.random.fold_in(rng, 6), axis_at), (parts,), jnp.float32, least / len(pieces), largest / len(pieces))
        return jnp.repeat(jnp.exp(draws), shape[axis_at] // parts).reshape((-1,) + (1,) * (len(shape) - axis_at - 1))

    gain = one(*pieces[0])
    for cut in pieces[1:]:
        gain = gain * one(*cut)
    return gain


def centred(key, dims, scale, reach, split=(), kind=jnp.bfloat16):
    factor_of = block_scale(key, dims, split, -0.22, 0.18) if split else 1.0
    array = jax.random.normal(key, dims, jnp.float32) * scale * factor_of
    return jnp.minimum(jnp.maximum(array, -reach), reach).astype(kind)


def heavy_noise(rng, extent, width, most, pieces, heavy, held_as=jnp.bfloat16):
    entries = width * jax.random.normal(rng, extent, jnp.float32)
    if pieces:
        entries = entries * block_scale(rng, extent, pieces, -0.22, 0.18)
    return jnp.clip(strengthened(entries, jax.random.fold_in(rng, 3), *heavy), -most, most).astype(held_as)


def setup_inputs(seed: int = 0) -> dict:
    streams_of = jax.random.split(jax.random.key(seed), 5)
    grad_out = heavy_noise(streams_of[0], (TOKENS, D), 1.0, 6.0, ((0, 8), (1, 16)), (1, 0, 16, 2.0))
    gate_act = centred(streams_of[1], (TOKENS, F), 1.5, 8.0, ((0, 16), (1, 8)))
    up_act = centred(streams_of[2], (TOKENS, F), 1.0, 6.0, ((0, 16), (1, 8)))
    down_weight = centred(streams_of[3], (F, D), D ** -0.5, 0.046875, ((0, 8), (1, 16)))
    return {"grad_out": grad_out, "gate_act": gate_act, "up_act": up_act, "down_weight": down_weight}


def reference(grad_out, gate_act, up_act, down_weight):
    gate_val = gate_act.astype(jnp.float32)
    up_val = up_act.astype(jnp.float32)
    sigmoid_g = jax.nn.sigmoid(gate_val)
    act_val = gate_val * sigmoid_g
    hidden = (act_val * up_val).astype(jnp.bfloat16)
    grad_hidden = lax.dot_general(grad_out, down_weight, (((1,), (1,)), ((), ())), preferred_element_type=jnp.float32)
    grad_gate = (grad_hidden * up_val * sigmoid_g * (1.0 + gate_val * (1.0 - sigmoid_g))).astype(jnp.bfloat16)
    grad_up = (grad_hidden * act_val).astype(jnp.bfloat16)
    grad_down = lax.dot_general(hidden, grad_out, (((0,), (0,)), ((), ())), preferred_element_type=jnp.float32).astype(jnp.bfloat16)
    return grad_gate, grad_up, grad_down
```

```python
import functools

import jax
import jax.numpy as jnp
from jax import lax
from jax.experimental import pallas as pl
from jax.experimental.pallas import tpu as pltpu
from jax.sharding import PartitionSpec as P

MESH = pl.DeviceIdType.MESH
BF = jnp.bfloat16
F32 = jnp.float32
NT = (((1,), (1,)), ((), ()))
NN = (((1,), (0,)), ((), ()))

TB = 256
DB = 1024
FH = 1664
RA = 1024
RB = FH - RA
HB = RB // 2
A = pl.ds(0, RA)
B = pl.ds(RA, RB)
B0 = pl.ds(RA, HB)
B1 = pl.ds(RA + HB, HB)
MT = 832
NTILE = 256


def at(i, size):
    return pl.ds(pl.multiple_of(i * size, size), size)


def kernel(dy_ref, gate_ref, up_ref, w_ref, gg_ref, gu_ref, gd_ref,
           wv, dyv, ht, g, u, part, r1p, r1m, r2pc, r2ps, r2mc, r2ms, ry, by, b1p, b1m, b2p, b2m,
           gdv, og, ou, ss, rs, ls):
    row, col = lax.axis_index("row"), lax.axis_index("col")
    yl, x, q = row // 8, (row // 2) % 4, row % 2
    z, yh = col // 2, col % 2
    o = 1 - q

    def dev(yl, x, q, z, yh):
        return {"row": (yl * 4 + x) * 2 + q, "col": z * 2 + yh}

    core = dev(yl, x, o, z, yh)
    xp = dev(yl, (x + 1) % 4, q, z, yh)
    xm = dev(yl, (x + 3) % 4, q, z, yh)
    ylp = dev(1 - yl, x, q, z, yh)
    zp = dev(yl, x, q, (z + 1) % 4, yh)
    zm = dev(yl, x, q, (z + 3) % 4, yh)
    yhp = dev(yl, x, q, z, 1 - yh)

    ids = {}

    def remote(name, src, dst, to):
        i = ids.setdefault(name, len(ids))
        return pltpu.make_async_remote_copy(src, dst, ss.at[i], rs.at[i], device_id=to, device_id_type=MESH)

    def cb(dz, fl):
        return ((z + dz) % 4) * 2 + (yh + fl) % 2

    def dyb(p, dz, fl):
        return dyv.at[p, at(cb(dz, fl), TB), :]

    def kb(fl, dx):
        return ((yl + fl) % 2) * 4 + (x + dx) % 4

    def htb(rows, fl, dx):
        return ht.at[rows, at(kb(fl, dx), TB)]

    def pt(fl, dx, rows):
        return part.at[kb(fl, dx), rows, :]

    def same(name, ref, to):
        return remote(name, ref, ref, to)

    half_q, half_o = at(q, FH), at(o, FH)
    tok_q, tok_o = at(q, 128), at(o, 128)

    D = {
        "G": remote("G", gate_ref.at[:, half_o], g.at[tok_q, :], core),
        "U": remote("U", up_ref.at[:, half_o], u.at[tok_q, :], core),
        "D1": remote("D1", dy_ref, dyb(q, 0, 0), core),
        "D2": remote("D2", dy_ref, dyb(q, 0, 0), yhp),
        "D3": remote("D3", dy_ref, dyb(q, 0, 0), zp),
        "D4": remote("D4", dy_ref, dyb(q, 0, 0), zm),
        "W": remote("W", w_ref.at[half_o, :], wv.at[q], core),
        "D5": same("D5", dyb(q, 3, 0), zp),
        "D6": same("D6", dyb(q, 0, 1), zp),
        "D7": same("D7", dyb(q, 0, 1), zm),
        "D8": same("D8", dyb(q, 1, 1), zm),
        "HA1": same("HA1", htb(A, 0, 0), xp),
        "HA2": same("HA2", htb(A, 0, 0), xm),
        "HB1": same("HB1", htb(B, 0, 0), xp),
        "HB2": same("HB2", htb(B, 0, 0), xm),
        "HYA": same("HYA", htb(A, 0, 0), ylp),
        "HYB": same("HYB", htb(B, 0, 0), ylp),
        "HB3": same("HB3", htb(B0, 0, 3), xp),
        "HB4": same("HB4", htb(B1, 0, 1), xm),
        "HYB2": same("HYB2", htb(B, 0, 3), ylp),
        "HYB3": same("HYB3", htb(B, 0, 1), ylp),
        "HYB4": same("HYB4", htb(B0, 0, 2), ylp),
        "HYB5": same("HYB5", htb(B1, 0, 2), ylp),
        "HA3": same("HA3", htb(A, 1, 0), xp),
        "HA4": same("HA4", htb(A, 1, 0), xm),
        "HA5": same("HA5", htb(A, 0, 3), xp),
        "HA6": same("HA6", htb(A, 1, 1), xm),
        "S1P": remote("S1P", pt(0, 2, A), r1p, xp),
        "S1M": remote("S1M", pt(1, 2, A), r1m, xm),
        "S2PS": remote("S2PS", pt(1, 1, A), r2ps, xp),
        "S2MS": remote("S2MS", pt(0, 3, A), r2ms, xm),
        "S2PC": remote("S2PC", pt(0, 1, A), r2pc, xp),
        "S2MC": remote("S2MC", pt(1, 3, A), r2mc, xm),
        "SYA": remote("SYA", pt(1, 0, A), ry, ylp),
        "SB1P": remote("SB1P", pt(0, 2, B0), b1p, xp),
        "SB1M": remote("SB1M", pt(0, 2, B1), b1m, xm),
        "SB2P": remote("SB2P", pt(0, 1, B), b2p, xp),
        "SB2M": remote("SB2M", pt(0, 3, B), b2m, xm),
    }
    for dx in range(4):
        D[f"SYB{dx}"] = remote(f"SYB{dx}", pt(1, dx, B), by.at[(x + dx) % 4], ylp)
    for dz, fl in ((3, 0), (1, 0), (0, 1), (2, 0), (1, 1), (3, 1), (2, 1)):
        D[f"C{dz}{fl}"] = same(f"C{dz}{fl}", dyb(q, dz, fl), core)
    for m in range(2):
        D[f"GD{m}"] = remote(f"GD{m}", gdv.at[o, pl.ds(m * MT, MT), :],
                             gd_ref.at[pl.ds(pl.multiple_of(q * FH + m * MT, MT), MT), :], core)
    for name, start, size in (("A", 0, RA), ("B", RA, RB)):
        there = pl.ds(pl.multiple_of(q * FH + start, 128), size)
        here = pl.ds(start, size)
        D["OG" + name] = remote("OG" + name, og.at[tok_o, here], gg_ref.at[:, there], core)
        D["OU" + name] = remote("OU" + name, ou.at[tok_o, here], gu_ref.at[:, there], core)

    def go(*names):
        for n in names:
            D[n].start()

    def got(*names):
        for n in names:
            D[n].wait_recv()

    local = {
        "g": pltpu.make_async_copy(gate_ref.at[:, half_q], g.at[tok_q, :], ls.at[0]),
        "u": pltpu.make_async_copy(up_ref.at[:, half_q], u.at[tok_q, :], ls.at[1]),
        "dy": pltpu.make_async_copy(dy_ref, dyb(q, 0, 0), ls.at[2]),
        "w": pltpu.make_async_copy(w_ref.at[half_q, :], wv.at[q], ls.at[3]),
    }
    for n in ("g", "u", "dy", "w"):
        local[n].start()

    bar = pltpu.get_barrier_semaphore()
    for to in (core, xp, xm, ylp, zp, zm, yhp):
        pl.semaphore_signal(bar, inc=1, device_id=to, device_id_type=MESH)
    pl.semaphore_wait(bar, 7)

    go("G", "U", "D2", "D3", "D4", "D1", "W")

    local["g"].wait()
    local["u"].wait()
    got("G", "U")

    def hidden(i, _):
        s = at(i, 128)
        gv, uv = g[:, s].astype(F32), u[:, s].astype(F32)
        h = gv * jax.nn.sigmoid(gv) * uv
        ht[s, at(kb(0, 0), TB)] = h.T.astype(BF)
        return 0

    lax.fori_loop(0, FH // 128, hidden, 0)
    go("HYA", "HB1", "HB2", "HA1", "HA2", "HYB")

    order = ((0, 0), (3, 0), (1, 0), (0, 1), (2, 0), (1, 1), (3, 1), (2, 1))

    def serve1(s):
        if s == 0:
            local["dy"].wait()
            local["w"].wait()
            got("W", "D1")
        elif s == 1:
            got("D3")
            go("D5", "C30")
            got("D4")
            go("C10")
            got("D2")
            go("D7", "D6", "C01")
            got("C30")
        elif s == 2:
            got("HB1", "HB2")
            go("HB3", "HB4", "HYB2", "HYB3")
            got("C10")
        elif s == 3:
            got("HA1", "HA2", "HYA")
            go("HA5", "HA4", "HA3")
            got("C01")
        elif s == 4:
            got("D5")
            go("C20")
            got("D7")
            go("D8", "C11")
            got("HB3", "HB4")
            go("HYB4", "HYB5")
            got("C20")
        elif s == 5:
            got("C11")
        elif s == 6:
            got("D6")
            go("C31")
            got("HA4")
            go("HA6")
            got("D8")
            go("C21")
            got("C31")
        elif s == 7:
            got("C21")

    def step1(s, _):
        for i in range(8):
            pl.when(s == i)(functools.partial(serve1, i))
        dz = fl = jnp.int32(0)
        for i, (a, b) in enumerate(order):
            dz = jnp.where(s == i, a, dz)
            fl = jnp.where(s == i, b, fl)
        c = cb(dz, fl)

        def tile(m, _):
            rows = at(m, MT)
            acc = None
            for p in range(2):
                d = lax.dot_general(wv[p, rows, :], dyv[p, at(c, TB), :], NT, preferred_element_type=F32)
                acc = d if acc is None else acc + d
            part[c, rows, :] = acc.astype(BF)
            return 0

        lax.fori_loop(0, FH // MT, tile, 0)
        return 0

    lax.fori_loop(0, 8, step1, 0)

    go("S1P", "S1M", "S2PS", "S2MS", "SYB2", "SYB1", "SYB3", "SYB0")

    def add(k, start, size, *others):
        def chunk(i, _):
            t = part[k, pl.ds(pl.multiple_of(start + i * 64, 64), 64), :].astype(F32)
            for ref, off in others:
                t = t + ref[pl.ds(pl.multiple_of(off + i * 64, 64), 64), :].astype(F32)
            part[k, pl.ds(pl.multiple_of(start + i * 64, 64), 64), :] = t.astype(BF)
            return 0

        lax.fori_loop(0, size // 64, chunk, 0)

    def serve2(s):
        if s == 0:
            got("HYB", "HYB2", "HYB3", "HYB4", "HYB5", "HA3", "HA5", "HA6")
        elif s == 8:
            got("S1P", "S1M")
            add(kb(0, 1), 0, RA, (r1p, 0))
            go("S2PC")
            add(kb(1, 3), 0, RA, (r1m, 0))
            go("S2MC")
            got("SYB2")
            add(kb(0, 2), RA, RB, (by.at[(x + 2) % 4], 0))
            go("SB1P", "SB1M", "GD0", "GD1")

    def step2(s, _):
        for i in (0, 8):
            pl.when(s == i)(functools.partial(serve2, i))
        p = jnp.where(s < 8, o, q)
        m = (s // 4) % 2
        n = s % 4
        rows, cols = at(m, MT), at(n, NTILE)
        d = lax.dot_general(ht[rows, :], dyv[p, :, cols], NN, preferred_element_type=F32)
        gdv[p, rows, cols] = d.astype(BF)
        return 0

    lax.fori_loop(0, 16, step2, 0)

    gd_out = pltpu.make_async_copy(gdv.at[q], gd_ref.at[half_q, :], ls.at[0])
    gd_out.start()

    got("SYB1", "SYB3", "SYB0")
    add(kb(0, 1), RA, RB, (by.at[(x + 1) % 4], 0))
    add(kb(0, 3), RA, RB, (by.at[(x + 3) % 4], 0))
    got("SB1P")
    add(kb(0, 1), RA, HB, (b1p, 0))
    go("SB2P")
    got("SB1M")
    add(kb(0, 3), RA + HB, HB, (b1m, 0))
    go("SB2M")

    got("S2PS", "S2MC", "S2PC", "S2MS")
    add(kb(1, 0), 0, RA, (r2ps, 0), (r2mc, 0))
    go("SYA")

    def final(first, last, *others):
        def tile(i, _):
            s = at(i, 128)
            t = part[kb(0, 0), s, :].astype(F32)
            for ref in others:
                t = t + ref[at(i - first, 128), :].astype(F32)
            gh = t.T
            gv, uv = g[:, s].astype(F32), u[:, s].astype(F32)
            sig = jax.nn.sigmoid(gv)
            og[:, s] = (gh * uv * sig * (1.0 + gv * (1.0 - sig))).astype(BF)
            ou[:, s] = (gh * (gv * sig)).astype(BF)
            return 0

        lax.fori_loop(first, last, tile, 0)

    outs = [gd_out]

    def emit(name, start, size, i):
        go("OG" + name, "OU" + name)
        there = pl.ds(pl.multiple_of(q * FH + start, 128), size)
        for ref, dst in ((og, gg_ref), (ou, gu_ref)):
            c = pltpu.make_async_copy(ref.at[tok_q, pl.ds(start, size)], dst.at[:, there], ls.at[i])
            c.start()
            outs.append(c)
            i += 1

    got("SB2P", "SB2M")
    final(RA // 128, FH // 128, by.at[x], b2p, b2m)
    emit("B", RA, RB, 1)
    got("SYA")
    final(0, RA // 128, r2pc, r2ms, ry)
    emit("A", 0, RA, 3)

    for c in outs:
        c.wait()
    got("GD0", "GD1", "OGA", "OUA", "OGB", "OUB")
    for n in D:
        D[n].wait_send()


def local(grad_out, gate_act, up_act, down_weight):
    hbm = pl.BlockSpec(memory_space=pl.ANY)
    block = lambda *s: pltpu.VMEM(s, BF)
    return pl.pallas_call(
        kernel,
        out_shape=(
            jax.ShapeDtypeStruct(gate_act.shape, BF),
            jax.ShapeDtypeStruct(up_act.shape, BF),
            jax.ShapeDtypeStruct(down_weight.shape, BF),
        ),
        in_specs=[hbm] * 4,
        out_specs=(hbm,) * 3,
        scratch_shapes=[
            block(2, FH, DB), block(2, 8 * TB, DB), block(FH, 8 * TB), block(TB, FH), block(TB, FH),
            block(8, FH, TB),
            block(RA, TB), block(RA, TB), block(RA, TB), block(RA, TB), block(RA, TB), block(RA, TB), block(RA, TB),
            block(4, RB, TB), block(HB, TB), block(HB, TB), block(RB, TB), block(RB, TB),
            block(2, FH, DB), block(TB, FH), block(TB, FH),
            pltpu.SemaphoreType.DMA((60,)), pltpu.SemaphoreType.DMA((60,)), pltpu.SemaphoreType.DMA((8,)),
        ],
        compiler_params=pltpu.CompilerParams(
            collective_id=0, has_side_effects=True, vmem_limit_bytes=60 * 2**20
        ),
        name="swiglu_down_backward",
    )(grad_out, gate_act, up_act, down_weight)


def solution(mesh):
    return jax.shard_map(
        local,
        mesh=mesh,
        in_specs=(P("col", "row"), P("row", "col"), P("row", "col"), P("col", "row")),
        out_specs=(P("row", "col"), P("row", "col"), P("col", "row")),
        check_vma=False,
    )
```

```python
import functools

import jax
import jax.numpy as jnp
from jax import lax
from jax.experimental import pallas as pl
from jax.experimental.pallas import tpu as pltpu
from jax.sharding import PartitionSpec as P

MESH = pl.DeviceIdType.MESH
BF = jnp.bfloat16
F32 = jnp.float32
NT = (((1,), (1,)), ((), ()))
NN = (((1,), (0,)), ((), ()))

TB = 256
DB = 1024
FH = 1664
RA = 1024
RB = FH - RA
HA = RA // 2
HB = RB // 2
HT = TB // 2
A = pl.ds(0, RA)
A0 = pl.ds(0, HA)
A1 = pl.ds(HA, HA)
B = pl.ds(RA, RB)
B0 = pl.ds(RA, HB)
B1 = pl.ds(RA + HB, HB)
MT = 832
NTILE = 256


def at(i, size):
    return pl.ds(pl.multiple_of(i * size, size), size)


def kernel(dy_ref, gate_ref, up_ref, w_ref, gg_ref, gu_ref, gd_ref,
           wv, dyv, ht, hs, gv, uv, gp, upv, part, r1p, r1m, r2pc, r2ps, r2mc, r2ms, ry, by, b1p, b1m, b2p, b2m,
           gdv, og, ou, ss, rs, ls):
    row, col = lax.axis_index("row"), lax.axis_index("col")
    yl, x, q = row // 8, (row // 2) % 4, row % 2
    z, yh = col // 2, col % 2
    o = 1 - q

    def dev(yl, x, q, z, yh):
        return {"row": (yl * 4 + x) * 2 + q, "col": z * 2 + yh}

    core = dev(yl, x, o, z, yh)
    xp = dev(yl, (x + 1) % 4, q, z, yh)
    xm = dev(yl, (x + 3) % 4, q, z, yh)
    ylp = dev(1 - yl, x, q, z, yh)
    zp = dev(yl, x, q, (z + 1) % 4, yh)
    zm = dev(yl, x, q, (z + 3) % 4, yh)
    yhp = dev(yl, x, q, z, 1 - yh)

    ids = {}

    def remote(name, src, dst, to):
        i = ids.setdefault(name, len(ids))
        return pltpu.make_async_remote_copy(src, dst, ss.at[i], rs.at[i], device_id=to, device_id_type=MESH)

    def cb(dz, fl):
        return ((z + dz) % 4) * 2 + (yh + fl) % 2

    def dyb(p, dz, fl):
        return dyv.at[p, at(cb(dz, fl), TB), :]

    def dyh(dz, fl, half):
        return dyv.at[q, at(cb(dz, fl) * 2 + half, HT), :]

    def kb(fl, dx):
        return ((yl + fl) % 2) * 4 + (x + dx) % 4

    def htb(rows, fl, dx):
        return ht.at[rows, at(kb(fl, dx), TB)]

    def hth(rows, core_of):
        return ht.at[rows, at(kb(0, 0) * 2 + core_of, HT)]

    def pt(fl, dx, rows):
        return part.at[kb(fl, dx), rows, :]

    def same(name, ref, to):
        return remote(name, ref, ref, to)

    half_q, half_o = at(q, FH), at(o, FH)

    D = {
        "HS": remote("HS", hs, hth(pl.ds(0, FH), q), core),
        "G": remote("G", gate_ref.at[:, half_o], gp, core),
        "U": remote("U", up_ref.at[:, half_o], upv, core),
        "D1": remote("D1", dy_ref, dyb(q, 0, 0), core),
        "D2": remote("D2", dy_ref, dyb(q, 0, 0), yhp),
        "D3": remote("D3", dy_ref, dyb(q, 0, 0), zp),
        "D4": remote("D4", dy_ref, dyb(q, 0, 0), zm),
        "W": remote("W", w_ref.at[half_o, :], wv.at[q], core),
        "D5a": same("D5a", dyh(3, 0, 0), zp),
        "D5b": same("D5b", dyh(1, 0, 1), zm),
        "D6": same("D6", dyb(q, 0, 1), zp),
        "D7": same("D7", dyb(q, 0, 1), zm),
        "D8a": same("D8a", dyh(3, 1, 0), zp),
        "D8b": same("D8b", dyh(1, 1, 1), zm),
        "HB1a": same("HB1a", hth(B, q), xp),
        "HB1b": same("HB1b", hth(B, o), xp),
        "HB2a": same("HB2a", hth(B, q), xm),
        "HB2b": same("HB2b", hth(B, o), xm),
        "HA1": same("HA1", htb(A, 0, 0), xp),
        "HA2": same("HA2", htb(A, 0, 0), xm),
        "HYA": same("HYA", htb(A, 0, 0), ylp),
        "HYB": same("HYB", htb(B, 0, 0), ylp),
        "HB3": same("HB3", htb(B0, 0, 3), xp),
        "HB4": same("HB4", htb(B1, 0, 1), xm),
        "HYB2": same("HYB2", htb(B, 0, 3), ylp),
        "HYB3": same("HYB3", htb(B, 0, 1), ylp),
        "HYB4": same("HYB4", htb(B0, 0, 2), ylp),
        "HYB5": same("HYB5", htb(B1, 0, 2), ylp),
        "HA3a": same("HA3a", htb(A0, 1, 0), xp),
        "HA3b": same("HA3b", htb(A1, 1, 0), xp),
        "HA4a": same("HA4a", htb(A0, 1, 0), xm),
        "HA4b": same("HA4b", htb(A1, 1, 0), xm),
        "HA5a": same("HA5a", htb(A0, 0, 3), xp),
        "HA5b": same("HA5b", htb(A1, 0, 1), xm),
        "HA6a": same("HA6a", htb(A0, 1, 3), xp),
        "HA6b": same("HA6b", htb(A1, 1, 1), xm),
        "S1P": remote("S1P", pt(0, 2, A), r1p, xp),
        "S1M": remote("S1M", pt(1, 2, A), r1m, xm),
        "SB1P": remote("SB1P", pt(0, 2, B0), b1p, xp),
        "SB1M": remote("SB1M", pt(0, 2, B1), b1m, xm),
        "SB2Pi": remote("SB2Pi", pt(0, 1, B1), b2p.at[pl.ds(HB, HB), :], xp),
        "SB2Pd": remote("SB2Pd", pt(0, 1, B0), b2p.at[pl.ds(0, HB), :], xp),
        "SB2Mi": remote("SB2Mi", pt(0, 3, B0), b2m.at[pl.ds(0, HB), :], xm),
        "SB2Md": remote("SB2Md", pt(0, 3, B1), b2m.at[pl.ds(HB, HB), :], xm),
    }
    for i, r in enumerate((A0, A1)):
        D[f"S2PS{i}"] = remote(f"S2PS{i}", pt(1, 1, r), r2ps.at[r, :], xp)
        D[f"S2MS{i}"] = remote(f"S2MS{i}", pt(0, 3, r), r2ms.at[r, :], xm)
        D[f"S2PC{i}"] = remote(f"S2PC{i}", pt(0, 1, r), r2pc.at[r, :], xp)
        D[f"S2MC{i}"] = remote(f"S2MC{i}", pt(1, 3, r), r2mc.at[r, :], xm)
        D[f"SYA{i}"] = remote(f"SYA{i}", pt(1, 0, r), ry.at[r, :], ylp)
    for dx in range(4):
        D[f"SYB{dx}"] = remote(f"SYB{dx}", pt(1, dx, B), by.at[(x + dx) % 4], ylp)
    for dz, fl in ((3, 0), (1, 0), (0, 1), (2, 0), (1, 1), (3, 1), (2, 1)):
        D[f"C{dz}{fl}"] = same(f"C{dz}{fl}", dyb(q, dz, fl), core)
    for m in range(2):
        D[f"GD{m}"] = remote(f"GD{m}", gdv.at[pl.ds(m * MT, MT), :],
                             gd_ref.at[pl.ds(pl.multiple_of(q * FH + m * MT, MT), MT), :], core)
    for name, start, size in (("0", 0, HA), ("1", HA, HA), ("2", RA, RB)):
        there = pl.ds(pl.multiple_of(q * FH + start, 128), size)
        here = pl.ds(start, size)
        D["OG" + name] = remote("OG" + name, og.at[:, here], gg_ref.at[:, there], core)
        D["OU" + name] = remote("OU" + name, ou.at[:, here], gu_ref.at[:, there], core)

    def go(*names):
        for n in names:
            D[n].start()

    def got(*names):
        for n in names:
            D[n].wait_recv()

    local = {
        "g": pltpu.make_async_copy(gate_ref, gv, ls.at[0]),
        "u": pltpu.make_async_copy(up_ref, uv, ls.at[1]),
        "dy": pltpu.make_async_copy(dy_ref, dyb(q, 0, 0), ls.at[2]),
        "w": pltpu.make_async_copy(w_ref.at[half_q, :], wv.at[q], ls.at[3]),
    }

    bar = pltpu.get_barrier_semaphore()
    for to in (core, xp, xm, ylp, zp, zm, yhp):
        pl.semaphore_signal(bar, inc=1, device_id=to, device_id_type=MESH)
    for n in ("g", "u", "dy", "w"):
        local[n].start()

    def hidden(first, last, half, dst, lanes):
        def tile(i, _):
            s = at(i, 128)
            f = pl.ds(pl.multiple_of(half * FH + i * 128, 128), 128)
            gt, ut = gv[:, f].astype(F32), uv[:, f].astype(F32)
            h = gt * jax.nn.sigmoid(gt) * ut
            dst[s, lanes] = h.T.astype(BF)
            return 0

        lax.fori_loop(first, last, tile, 0)

    own = at(kb(0, 0) * 2 + q, HT)
    local["g"].wait()
    local["u"].wait()
    hidden(RA // 128, FH // 128, q, ht, own)
    pl.semaphore_wait(bar, 7)

    go("D2", "D3", "D4", "HB1a", "HB2a")
    hidden(0, FH // 128, o, hs, pl.ds(0, HT))
    go("HS")
    hidden(0, RA // 128, q, ht, own)
    go("D1", "W", "G", "U")
    got("HS")
    go("HYA", "HB1b", "HB2b", "HA1", "HA2", "HYB")

    order = ((0, 0), (3, 0), (1, 0), (0, 1), (3, 1), (1, 1), (2, 0), (2, 1))

    def serve1(s):
        if s == 0:
            got("HB1a", "HB2a", "HB1b", "HB2b")
            go("HB3", "HB4", "HYB2", "HYB3")
            got("D3", "D4", "D2")
            go("D6", "D7", "D5a", "D5b", "C30", "C10", "C01")
            local["dy"].wait()
            local["w"].wait()
            got("W", "D1")
        elif s == 1:
            got("C30")
        elif s == 2:
            got("C10")
        elif s == 3:
            got("HA1", "HA2")
            go("HA5a", "HA5b")
            got("HYA")
            go("HA3a", "HA4b", "HA3b", "HA4a")
            got("C01")
        elif s == 4:
            got("HB3", "HB4")
            go("HYB4", "HYB5")
            got("D6", "D7")
            go("D8a", "D8b", "C31", "C11")
            got("C31")
        elif s == 5:
            got("C11")
        elif s == 6:
            got("D5a", "D5b")
            go("C20")
            got("C20")
        elif s == 7:
            got("HA3a", "HA4b")
            go("HA6a", "HA6b")
            got("D8a", "D8b")
            go("C21")
            got("C21")

    def step1(s, _):
        for i in range(8):
            pl.when(s == i)(functools.partial(serve1, i))
        dz = fl = jnp.int32(0)
        for i, (a, b) in enumerate(order):
            dz = jnp.where(s == i, a, dz)
            fl = jnp.where(s == i, b, fl)
        c = cb(dz, fl)

        def tile(m, _):
            rows = at(m, MT)
            acc = None
            for p in range(2):
                d = lax.dot_general(wv[p, rows, :], dyv[p, at(c, TB), :], NT, preferred_element_type=F32)
                acc = d if acc is None else acc + d
            part[c, rows, :] = acc.astype(BF)
            return 0

        lax.fori_loop(0, FH // MT, tile, 0)
        return 0

    lax.fori_loop(0, 8, step1, 0)

    go("S1P", "S1M", "S2PS0", "S2MS0", "SYB2", "SYB1", "SYB3")

    def add(k, start, size, *others):
        def chunk(i, _):
            here = pl.ds(pl.multiple_of(start + i * 64, 64), 64)
            t = part[k, here, :].astype(F32)
            for ref, off in others:
                t = t + ref[pl.ds(pl.multiple_of(off + i * 64, 64), 64), :].astype(F32)
            part[k, here, :] = t.astype(BF)
            return 0

        lax.fori_loop(0, size // 64, chunk, 0)

    def serve2(s):
        if s == 0:
            got("HYB", "HYB2", "HYB3", "HYB4", "HYB5", "HA3b", "HA4a", "HA5a", "HA5b", "HA6a", "HA6b")
        elif s == 6:
            got("S1P", "S1M")
            add(kb(0, 1), 0, HA, (r1p, 0))
            add(kb(1, 3), 0, HA, (r1m, 0))
            go("S2PC0", "S2MC0", "S2PS1", "S2MS1")
            add(kb(0, 1), HA, HA, (r1p, HA))
            add(kb(1, 3), HA, HA, (r1m, HA))
            go("S2PC1", "S2MC1")
            got("SYB2")
            add(kb(0, 2), RA, RB, (by.at[(x + 2) % 4], 0))
            go("SB1P", "SB1M")
        elif s == 13:
            got("S2PS0", "S2MC0")
            add(kb(1, 0), 0, HA, (r2ps, 0), (r2mc, 0))
            go("SYA0", "SYB0", "GD0", "GD1")
            got("SYB1", "SYB3")
            add(kb(0, 1), RA, RB, (by.at[(x + 1) % 4], 0))
            add(kb(0, 3), RA, RB, (by.at[(x + 3) % 4], 0))
            go("SB2Pi", "SB2Mi")

    def step2(s, _):
        for i in (0, 6, 13):
            pl.when(s == i)(functools.partial(serve2, i))
        m = (s // 4) % 2
        rows, cols = at(m, MT), at(s % 4, NTILE)

        def tile(p):
            return lax.dot_general(ht[rows, :], dyv[p, :, cols], NN, preferred_element_type=F32).astype(BF)

        t = tile(jnp.where(s < 8, o, q))

        @pl.when(s < 8)
        def _():
            gdv[rows, cols] = t

        @pl.when(s >= 8)
        def _():
            gd_ref[pl.ds(pl.multiple_of(q * FH + m * MT, MT), MT), cols] = t

        return 0

    lax.fori_loop(0, 16, step2, 0)

    got("S2PS1", "S2MC1")
    add(kb(1, 0), HA, HA, (r2ps, HA), (r2mc, HA))
    go("SYA1")

    got("G", "U")

    def final(first, last, base, *others):
        def tile(i, _):
            s = at(i, 128)
            f = pl.ds(pl.multiple_of(q * FH + i * 128, 128), 128)
            for who, gr, ur, fi, dg, du, fo in ((q, gv, uv, f, gg_ref, gu_ref, f), (o, gp, upv, s, og, ou, s)):
                lanes = at(who, HT)
                t = part[kb(0, 0), s, lanes].astype(F32)
                for ref in others:
                    t = t + ref[at(i - base, 128), lanes].astype(F32)
                gh = t.T
                gt, ut = gr[:, fi].astype(F32), ur[:, fi].astype(F32)
                sig = jax.nn.sigmoid(gt)
                dg[:, fo] = (gh * ut * sig * (1.0 + gt * (1.0 - sig))).astype(BF)
                du[:, fo] = (gh * (gt * sig)).astype(BF)
            return 0

        lax.fori_loop(first, last, tile, 0)

    got("S2PC0", "S2MS0", "SYA0")
    final(0, HA // 128, 0, r2pc, r2ms, ry)
    go("OG0", "OU0")
    got("SB1P", "SB1M")
    add(kb(0, 1), RA, HB, (b1p, 0))
    add(kb(0, 3), RA + HB, HB, (b1m, 0))
    go("SB2Pd", "SB2Md")
    got("S2PC1", "S2MS1", "SYA1")
    final(HA // 128, RA // 128, 0, r2pc, r2ms, ry)
    go("OG1", "OU1")
    got("SYB0", "SB2Pi", "SB2Mi", "SB2Pd", "SB2Md")
    final(RA // 128, FH // 128, RA // 128, by.at[x], b2p, b2m)
    go("OG2", "OU2")

    got("GD0", "GD1", "OG0", "OU0", "OG1", "OU1", "OG2", "OU2")
    for n in D:
        D[n].wait_send()


def write_out(gg, gu, gd, gg_ref, gu_ref, gd_ref, sems):
    cs = [pltpu.make_async_copy(gg, gg_ref, sems.at[0]), pltpu.make_async_copy(gu, gu_ref, sems.at[1])]
    for i in range(2):
        rows = pl.ds(i * FH, FH)
        cs.append(pltpu.make_async_copy(gd.at[rows, :], gd_ref.at[rows, :], sems.at[2 + i]))
    for c in cs:
        c.start()
    for c in cs:
        c.wait()


def local(grad_out, gate_act, up_act, down_weight):
    hbm = pl.BlockSpec(memory_space=pltpu.HBM)
    vmem = pl.BlockSpec(memory_space=pltpu.VMEM)
    block = lambda *s: pltpu.VMEM(s, BF)
    shapes = (gate_act.shape, up_act.shape, down_weight.shape)
    held = pl.pallas_call(
        kernel,
        out_shape=tuple(block(*s) for s in shapes),
        in_specs=[hbm] * 4,
        out_specs=(vmem,) * 3,
        scratch_shapes=[
            block(2, FH, DB), block(2, 8 * TB, DB), block(FH, 8 * TB), block(FH, HT),
            block(HT, 2 * FH), block(HT, 2 * FH), block(HT, FH), block(HT, FH),
            block(8, FH, TB),
            block(RA, TB), block(RA, TB), block(RA, TB), block(RA, TB), block(RA, TB), block(RA, TB), block(RA, TB),
            block(4, RB, TB), block(HB, TB), block(HB, TB), block(RB, TB), block(RB, TB),
            block(FH, DB), block(HT, FH), block(HT, FH),
            pltpu.SemaphoreType.DMA((80,)), pltpu.SemaphoreType.DMA((80,)), pltpu.SemaphoreType.DMA((4,)),
        ],
        compiler_params=pltpu.CompilerParams(
            collective_id=0, has_side_effects=True, vmem_limit_bytes=52 * 2**20
        ),
        name="swiglu_down_backward",
    )(grad_out, gate_act, up_act, down_weight)
    return pl.pallas_call(
        write_out,
        out_shape=tuple(jax.ShapeDtypeStruct(s, BF) for s in shapes),
        in_specs=[vmem] * 3,
        out_specs=(hbm,) * 3,
        scratch_shapes=[pltpu.SemaphoreType.DMA((4,))],
        compiler_params=pltpu.CompilerParams(vmem_limit_bytes=10 * 2**20),
        name="write_out",
    )(*held)


def solution(mesh):
    return jax.shard_map(
        local,
        mesh=mesh,
        in_specs=(P("col", "row"), P("row", "col"), P("row", "col"), P("col", "row")),
        out_specs=(P("row", "col"), P("row", "col"), P("col", "row")),
        check_vma=False,
    )
```

```python
import functools

import jax
import jax.numpy as jnp
from jax import lax
from jax.experimental import pallas as pl
from jax.experimental.pallas import tpu as pltpu
from jax.sharding import PartitionSpec as P

MESH = pl.DeviceIdType.MESH
BF = jnp.bfloat16
F32 = jnp.float32
NT = (((1,), (1,)), ((), ()))
NN = (((1,), (0,)), ((), ()))

TB = 256
DB = 1024
FH = 1664
RA = 1024
RB = FH - RA
HA = RA // 2
HB = RB // 2
HT = TB // 2
A = pl.ds(0, RA)
A0 = pl.ds(0, HA)
A1 = pl.ds(HA, HA)
B = pl.ds(RA, RB)
B0 = pl.ds(RA, HB)
B1 = pl.ds(RA + HB, HB)
MT = 832
NTILE = 256


def at(i, size):
    return pl.ds(pl.multiple_of(i * size, size), size)


def kernel(dy_ref, gate_ref, up_ref, w_ref, gd_ref, tot, ry, b2p, b2m, fg, fu,
           wv, dyv, ht, hs, gv, uv, part, r1p, r1m, r2pc, r2ps, r2mc, r2ms, by, b1p, b1m, gdv, tots, ss, rs, ls):
    row, col = lax.axis_index("row"), lax.axis_index("col")
    yl, x, q = row // 8, (row // 2) % 4, row % 2
    z, yh = col // 2, col % 2
    o = 1 - q

    def dev(yl, x, q, z, yh):
        return {"row": (yl * 4 + x) * 2 + q, "col": z * 2 + yh}

    core = dev(yl, x, o, z, yh)
    xp = dev(yl, (x + 1) % 4, q, z, yh)
    xm = dev(yl, (x + 3) % 4, q, z, yh)
    ylp = dev(1 - yl, x, q, z, yh)
    zp = dev(yl, x, q, (z + 1) % 4, yh)
    zm = dev(yl, x, q, (z + 3) % 4, yh)
    yhp = dev(yl, x, q, z, 1 - yh)
    xpo = dev(yl, (x + 1) % 4, o, z, yh)
    xmo = dev(yl, (x + 3) % 4, o, z, yh)
    ylo = dev(1 - yl, x, o, z, yh)

    ids = {}

    def remote(name, src, dst, to):
        i = ids.setdefault(name, len(ids))
        return pltpu.make_async_remote_copy(src, dst, ss.at[i], rs.at[i], device_id=to, device_id_type=MESH)

    def cb(dz, fl):
        return ((z + dz) % 4) * 2 + (yh + fl) % 2

    def dyb(p, dz, fl):
        return dyv.at[p, at(cb(dz, fl), TB), :]

    def dyh(dz, fl, half):
        return dyv.at[q, at(cb(dz, fl) * 2 + half, HT), :]

    def kb(fl, dx):
        return ((yl + fl) % 2) * 4 + (x + dx) % 4

    def htb(rows, fl, dx):
        return ht.at[rows, at(kb(fl, dx), TB)]

    def hth(rows, core_of):
        return ht.at[rows, at(kb(0, 0) * 2 + core_of, HT)]

    def pt(fl, dx, rows):
        return part.at[kb(fl, dx), rows, :]

    def ptc(fl, dx, rows, core_of):
        return part.at[kb(fl, dx), rows, at(core_of, HT)]

    def same(name, ref, to):
        return remote(name, ref, ref, to)

    half_q, half_o = at(q, FH), at(o, FH)

    D = {
        "HS": remote("HS", hs, hth(pl.ds(0, FH), q), core),
        "D1": remote("D1", dy_ref, dyb(q, 0, 0), core),
        "D2": remote("D2", dy_ref, dyb(q, 0, 0), yhp),
        "D3": remote("D3", dy_ref, dyb(q, 0, 0), zp),
        "D4": remote("D4", dy_ref, dyb(q, 0, 0), zm),
        "W": remote("W", w_ref.at[half_o, :], wv.at[q], core),
        "D5a": same("D5a", dyh(3, 0, 0), zp),
        "D5b": same("D5b", dyh(1, 0, 1), zm),
        "D6": same("D6", dyb(q, 0, 1), zp),
        "D7": same("D7", dyb(q, 0, 1), zm),
        "D8a": same("D8a", dyh(3, 1, 0), zp),
        "D8b": same("D8b", dyh(1, 1, 1), zm),
        "HB1a": same("HB1a", hth(B, q), xp),
        "HB1b": same("HB1b", hth(B, o), xp),
        "HB2a": same("HB2a", hth(B, q), xm),
        "HB2b": same("HB2b", hth(B, o), xm),
        "HA1": same("HA1", htb(A, 0, 0), xp),
        "HA2": same("HA2", htb(A, 0, 0), xm),
        "HYA": same("HYA", htb(A, 0, 0), ylp),
        "HYB": same("HYB", htb(B, 0, 0), ylp),
        "HB3": same("HB3", htb(B0, 0, 3), xp),
        "HB4": same("HB4", htb(B1, 0, 1), xm),
        "HYB2": same("HYB2", htb(B, 0, 3), ylp),
        "HYB3": same("HYB3", htb(B, 0, 1), ylp),
        "HYB4": same("HYB4", htb(B0, 0, 2), ylp),
        "HYB5": same("HYB5", htb(B1, 0, 2), ylp),
        "HA3a": same("HA3a", htb(A0, 1, 0), xp),
        "HA3b": same("HA3b", htb(A1, 1, 0), xp),
        "HA4a": same("HA4a", htb(A0, 1, 0), xm),
        "HA4b": same("HA4b", htb(A1, 1, 0), xm),
        "HA5a": same("HA5a", htb(A0, 0, 3), xp),
        "HA5b": same("HA5b", htb(A1, 0, 1), xm),
        "HA6a": same("HA6a", htb(A0, 1, 3), xp),
        "HA6b": same("HA6b", htb(A1, 1, 1), xm),
        "S1P": remote("S1P", pt(0, 2, A), r1p, xp),
        "S1M": remote("S1M", pt(1, 2, A), r1m, xm),
        "SB1P": remote("SB1P", pt(0, 2, B0), b1p, xp),
        "SB1M": remote("SB1M", pt(0, 2, B1), b1m, xm),
    }
    for i, r in enumerate((A0, A1)):
        D[f"S2PS{i}"] = remote(f"S2PS{i}", pt(1, 1, r), r2ps.at[r, :], xp)
        D[f"S2MS{i}"] = remote(f"S2MS{i}", pt(0, 3, r), r2ms.at[r, :], xm)
        D[f"S2PC{i}"] = remote(f"S2PC{i}", pt(0, 1, r), r2pc.at[r, :], xp)
        D[f"S2MC{i}"] = remote(f"S2MC{i}", pt(1, 3, r), r2mc.at[r, :], xm)
        for who, to, c in (("s", ylp, q), ("x", ylo, o)):
            D[f"SYA{i}{who}"] = remote(f"SYA{i}{who}", ptc(1, 0, r, c), ry.at[q, r, :], to)
    for dx in range(4):
        D[f"SYB{dx}"] = remote(f"SYB{dx}", pt(1, dx, B), by.at[(x + dx) % 4], ylp)
    for dz, fl in ((3, 0), (1, 0), (0, 1), (2, 0), (1, 1), (3, 1), (2, 1)):
        D[f"C{dz}{fl}"] = same(f"C{dz}{fl}", dyb(q, dz, fl), core)
    for m in range(2):
        D[f"GD{m}"] = remote(f"GD{m}", gdv.at[pl.ds(m * MT, MT), :],
                             gd_ref.at[pl.ds(pl.multiple_of(q * FH + m * MT, MT), MT), :], core)
    for who, up_to, down_to, c in (("s", xp, xm, q), ("x", xpo, xmo, o)):
        for n, dx, rows, dst, first, to in (("SB2Pi", 1, B1, b2p, HB, up_to), ("SB2Pd", 1, B0, b2p, 0, up_to),
                                            ("SB2Mi", 3, B0, b2m, 0, down_to), ("SB2Md", 3, B1, b2m, HB, down_to)):
            D[n + who] = remote(n + who, ptc(0, dx, rows, c), dst.at[q, pl.ds(first, HB), :], to)
    for n, rows in (("TA", A), ("TB", B)):
        D[n] = remote(n, tots.at[rows, :], tot.at[q, rows, :], core)

    def go(*names):
        for n in names:
            D[n].start()

    def got(*names):
        for n in names:
            D[n].wait_recv()

    local = {
        "g": pltpu.make_async_copy(gate_ref, gv, ls.at[0]),
        "u": pltpu.make_async_copy(up_ref, uv, ls.at[1]),
        "dy": pltpu.make_async_copy(dy_ref, dyb(q, 0, 0), ls.at[2]),
        "w": pltpu.make_async_copy(w_ref.at[half_q, :], wv.at[q], ls.at[3]),
    }

    bar = pltpu.get_barrier_semaphore()
    for to in (core, xp, xm, ylp, zp, zm, yhp, xpo, xmo, ylo):
        pl.semaphore_signal(bar, inc=1, device_id=to, device_id_type=MESH)
    for n in ("g", "u", "dy", "w"):
        local[n].start()

    def hidden(first, last, half, dst, lanes):
        def tile(i, _):
            s = at(i, 128)
            f = pl.ds(pl.multiple_of(half * FH + i * 128, 128), 128)
            gt, ut = gv[:, f].astype(F32), uv[:, f].astype(F32)
            h = gt * jax.nn.sigmoid(gt) * ut
            dst[s, lanes] = h.T.astype(BF)
            return 0

        lax.fori_loop(first, last, tile, 0)

    own = at(kb(0, 0) * 2 + q, HT)
    local["g"].wait()
    local["u"].wait()
    hidden(RA // 128, FH // 128, q, ht, own)
    pl.semaphore_wait(bar, 10)

    go("D2", "D3", "D4", "HB1a", "HB2a")
    hidden(0, FH // 128, o, hs, pl.ds(0, HT))
    go("HS")
    hidden(0, RA // 128, q, ht, own)
    go("D1", "W")
    got("HS")
    go("HYA", "HB1b", "HB2b", "HA1", "HA2", "HYB")

    def factors(i, _):
        f = at(i, 128)
        gt, ut = gv[:, f].astype(F32), uv[:, f].astype(F32)
        sig = jax.nn.sigmoid(gt)
        fg[:, f] = ut * sig * (1.0 + gt * (1.0 - sig))
        fu[:, f] = gt * sig
        return 0

    order = ((0, 0), (3, 0), (1, 0), (0, 1), (3, 1), (1, 1), (2, 0), (2, 1))

    def serve1(s):
        if s == 0:
            got("HB1a", "HB2a", "HB1b", "HB2b")
            go("HB3", "HB4", "HYB2", "HYB3")
            got("D3", "D4", "D2")
            go("D6", "D7", "D5a", "D5b", "C30", "C10", "C01")
            local["dy"].wait()
            local["w"].wait()
            got("W", "D1")
        elif s == 1:
            got("C30")
        elif s == 2:
            lax.fori_loop(0, 2 * FH // 128, factors, 0)
            got("C10")
        elif s == 3:
            got("HA1", "HA2")
            go("HA5a", "HA5b")
            got("HYA")
            go("HA3a", "HA4b", "HA3b", "HA4a")
            got("C01")
        elif s == 4:
            got("HB3", "HB4")
            go("HYB4", "HYB5")
            got("D6", "D7")
            go("D8a", "D8b", "C31", "C11")
            got("C31")
        elif s == 5:
            got("C11")
        elif s == 6:
            got("D5a", "D5b")
            go("C20")
            got("C20")
        elif s == 7:
            got("HA3a", "HA4b")
            go("HA6a", "HA6b")
            got("D8a", "D8b")
            go("C21")
            got("C21")

    def step1(s, _):
        for i in range(8):
            pl.when(s == i)(functools.partial(serve1, i))
        dz = fl = jnp.int32(0)
        for i, (a, b) in enumerate(order):
            dz = jnp.where(s == i, a, dz)
            fl = jnp.where(s == i, b, fl)
        c = cb(dz, fl)

        def tile(m, _):
            rows = at(m, MT)
            acc = None
            for p in range(2):
                d = lax.dot_general(wv[p, rows, :], dyv[p, at(c, TB), :], NT, preferred_element_type=F32)
                acc = d if acc is None else acc + d
            part[c, rows, :] = acc.astype(BF)
            return 0

        lax.fori_loop(0, FH // MT, tile, 0)
        return 0

    lax.fori_loop(0, 8, step1, 0)

    go("S1P", "S1M", "S2PS0", "S2MS0", "SYB2", "SYB1", "SYB3")

    def add(k, start, size, *others):
        def chunk(i, _):
            here = pl.ds(pl.multiple_of(start + i * 64, 64), 64)
            t = part[k, here, :].astype(F32)
            for ref, off in others:
                t = t + ref[pl.ds(pl.multiple_of(off + i * 64, 64), 64), :].astype(F32)
            part[k, here, :] = t.astype(BF)
            return 0

        lax.fori_loop(0, size // 64, chunk, 0)

    def serve2(s):
        if s == 0:
            got("HYB", "HYB2", "HYB3", "HYB4", "HYB5", "HA3b", "HA4a", "HA5a", "HA5b", "HA6a", "HA6b")
        elif s == 6:
            got("S1P", "S1M")
            add(kb(0, 1), 0, HA, (r1p, 0))
            add(kb(1, 3), 0, HA, (r1m, 0))
            go("S2PC0", "S2MC0", "S2PS1", "S2MS1")
            add(kb(0, 1), HA, HA, (r1p, HA))
            add(kb(1, 3), HA, HA, (r1m, HA))
            go("S2PC1", "S2MC1")
            got("SYB2")
            add(kb(0, 2), RA, RB, (by.at[(x + 2) % 4], 0))
            go("SB1P", "SB1M")
        elif s == 13:
            got("S2PS0", "S2MC0")
            add(kb(1, 0), 0, HA, (r2ps, 0), (r2mc, 0))
            go("SYA0s", "SYA0x", "SYB0", "GD0", "GD1")
            got("SYB1", "SYB3")
            add(kb(0, 1), RA, RB, (by.at[(x + 1) % 4], 0))
            add(kb(0, 3), RA, RB, (by.at[(x + 3) % 4], 0))
            go("SB2Pis", "SB2Mis", "SB2Pix", "SB2Mix")

    def step2(s, _):
        for i in (0, 6, 13):
            pl.when(s == i)(functools.partial(serve2, i))
        m = (s // 4) % 2
        rows, cols = at(m, MT), at(s % 4, NTILE)

        def tile(p):
            return lax.dot_general(ht[rows, :], dyv[p, :, cols], NN, preferred_element_type=F32).astype(BF)

        t = tile(jnp.where(s < 8, o, q))

        @pl.when(s < 8)
        def _():
            gdv[rows, cols] = t

        @pl.when(s >= 8)
        def _():
            gd_ref[pl.ds(pl.multiple_of(q * FH + m * MT, MT), MT), cols] = t

        return 0

    lax.fori_loop(0, 16, step2, 0)

    got("S2PS1", "S2MC1")
    add(kb(1, 0), HA, HA, (r2ps, HA), (r2mc, HA))
    go("SYA1s", "SYA1x")
    got("SB1P", "SB1M")
    add(kb(0, 1), RA, HB, (b1p, 0))
    add(kb(0, 3), RA + HB, HB, (b1m, 0))
    go("SB2Pds", "SB2Mds", "SB2Pdx", "SB2Mdx")

    def total(start, size, *others):
        def chunk(i, _):
            here = pl.ds(pl.multiple_of(start + i * 64, 64), 64)
            off = at(i, 64)
            for c, dst in ((q, tot.at[q]), (o, tots)):
                lanes = at(c, HT)
                t = part[kb(0, 0), here, lanes].astype(F32)
                for ref in others:
                    t = t + ref[off, lanes].astype(F32)
                dst[here, :] = t
            return 0

        lax.fori_loop(0, size // 64, chunk, 0)

    got("S2PC0", "S2MS0", "S2PC1", "S2MS1")
    total(0, RA, r2pc, r2ms)
    go("TA")
    got("SYB0")
    total(RA, RB, by.at[x])
    go("TB")

    got("GD0", "GD1", "TA", "TB", "SYA0s", "SYA0x", "SYA1s", "SYA1x")
    for n in D:
        if n.startswith("SB2"):
            D[n].wait_recv()
    for n in D:
        D[n].wait_send()


def finish(gd, tot, ry, b2p, b2m, fg, fu, gg_ref, gu_ref, gd_ref, og, ou, sems):
    cs = []

    def put(src, dst):
        c = pltpu.make_async_copy(src, dst, sems.at[len(cs)])
        c.start()
        cs.append(c)

    for h in range(2):
        rows = pl.ds(h * FH, FH)
        put(gd.at[rows, :], gd_ref.at[rows, :])
    for h in range(2):
        def tile(first, *others):
            def body(i, _):
                s = at(i, 128)
                f = pl.ds(pl.multiple_of(h * FH + i * 128, 128), 128)
                t = tot[h, s, :]
                for ref in others:
                    t = t + ref[h, at(i - first, 128), :].astype(F32)
                gh = t.T
                og[:, f] = (gh * fg[:, f]).astype(BF)
                ou[:, f] = (gh * fu[:, f]).astype(BF)
                return 0

            return body

        lax.fori_loop(0, RA // 128, tile(0, ry), 0)
        lax.fori_loop(RA // 128, FH // 128, tile(RA // 128, b2p, b2m), 0)
        cols = pl.ds(h * FH, FH)
        put(og.at[:, cols], gg_ref.at[:, cols])
        put(ou.at[:, cols], gu_ref.at[:, cols])
    for c in cs:
        c.wait()


def local(grad_out, gate_act, up_act, down_weight):
    hbm = pl.BlockSpec(memory_space=pltpu.HBM)
    vmem = pl.BlockSpec(memory_space=pltpu.VMEM)
    block = lambda *s: pltpu.VMEM(s, BF)
    wide = lambda *s: pltpu.VMEM(s, F32)
    tokens, weight = gate_act.shape, down_weight.shape
    held = pl.pallas_call(
        kernel,
        out_shape=(
            block(*weight), wide(2, FH, HT), block(2, RA, HT), block(2, RB, HT), block(2, RB, HT),
            wide(*tokens), wide(*tokens),
        ),
        in_specs=[hbm] * 4,
        out_specs=(vmem,) * 7,
        scratch_shapes=[
            block(2, FH, DB), block(2, 8 * TB, DB), block(FH, 8 * TB), block(FH, HT),
            block(HT, 2 * FH), block(HT, 2 * FH),
            block(8, FH, TB),
            block(RA, TB), block(RA, TB), block(RA, TB), block(RA, TB), block(RA, TB), block(RA, TB),
            block(4, RB, TB), block(HB, TB), block(HB, TB),
            block(FH, DB), wide(FH, HT),
            pltpu.SemaphoreType.DMA((90,)), pltpu.SemaphoreType.DMA((90,)), pltpu.SemaphoreType.DMA((4,)),
        ],
        compiler_params=pltpu.CompilerParams(
            collective_id=0, has_side_effects=True, vmem_limit_bytes=46 * 2**20
        ),
        name="swiglu_down_backward",
    )(grad_out, gate_act, up_act, down_weight)
    return pl.pallas_call(
        finish,
        out_shape=tuple(jax.ShapeDtypeStruct(s, BF) for s in (tokens, tokens, weight)),
        in_specs=[vmem] * 7,
        out_specs=(hbm,) * 3,
        scratch_shapes=[block(*tokens), block(*tokens), pltpu.SemaphoreType.DMA((6,))],
        compiler_params=pltpu.CompilerParams(vmem_limit_bytes=6 * 2**20),
        name="finish",
    )(*held)


def solution(mesh):
    return jax.shard_map(
        local,
        mesh=mesh,
        in_specs=(P("col", "row"), P("row", "col"), P("row", "col"), P("col", "row")),
        out_specs=(P("row", "col"), P("row", "col"), P("col", "row")),
        check_vma=False,
    )
```

```python
import functools

import jax
import jax.numpy as jnp
from jax import lax
from jax.experimental import pallas as pl
from jax.experimental.pallas import tpu as pltpu
from jax.sharding import PartitionSpec as P

MESH = pl.DeviceIdType.MESH
BF = jnp.bfloat16
F32 = jnp.float32
NT = (((1,), (1,)), ((), ()))
NN = (((1,), (0,)), ((), ()))

TB = 256
DB = 1024
FH = 1664
RA = 1024
RB = FH - RA
HA = RA // 2
HB = RB // 2
HT = TB // 2
A = pl.ds(0, RA)
A0 = pl.ds(0, HA)
A1 = pl.ds(HA, HA)
B = pl.ds(RA, RB)
B0 = pl.ds(RA, HB)
B1 = pl.ds(RA + HB, HB)
GA = 1056
GB = FH - GA
GHA = GA // 2
GHB = GB // 2
GA_ = pl.ds(0, GA)
GA0 = pl.ds(0, GHA)
GA1 = pl.ds(GHA, GHA)
GB_ = pl.ds(GA, GB)
GB0 = pl.ds(GA, GHB)
GB1 = pl.ds(GA + GHB, GHB)
MT = 832
NTILE = 256


def at(i, size):
    return pl.ds(pl.multiple_of(i * size, size), size)


def kernel(dy_ref, gate_ref, up_ref, w_ref, gd_ref, tot, ry, b2p, b2m, fg, fu,
           wv, dyv, ht, hs, gv, uv, part, r1p, r1m, r2pc, r2ps, r2mc, r2ms, by, b1p, b1m, gdv, tots, ss, rs, ls):
    row, col = lax.axis_index("row"), lax.axis_index("col")
    yl, x, q = row // 8, (row // 2) % 4, row % 2
    z, yh = col // 2, col % 2
    o = 1 - q

    def dev(yl, x, q, z, yh):
        return {"row": (yl * 4 + x) * 2 + q, "col": z * 2 + yh}

    core = dev(yl, x, o, z, yh)
    xp = dev(yl, (x + 1) % 4, q, z, yh)
    xm = dev(yl, (x + 3) % 4, q, z, yh)
    ylp = dev(1 - yl, x, q, z, yh)
    zp = dev(yl, x, q, (z + 1) % 4, yh)
    zm = dev(yl, x, q, (z + 3) % 4, yh)
    yhp = dev(yl, x, q, z, 1 - yh)
    xpo = dev(yl, (x + 1) % 4, o, z, yh)
    xmo = dev(yl, (x + 3) % 4, o, z, yh)
    ylo = dev(1 - yl, x, o, z, yh)

    ids = {}

    def remote(name, src, dst, to):
        i = ids.setdefault(name, len(ids))
        return pltpu.make_async_remote_copy(src, dst, ss.at[i], rs.at[i], device_id=to, device_id_type=MESH)

    def cb(dz, fl):
        return ((z + dz) % 4) * 2 + (yh + fl) % 2

    def dyb(p, dz, fl):
        return dyv.at[p, at(cb(dz, fl), TB), :]

    def dyh(dz, fl, half):
        return dyv.at[q, at(cb(dz, fl) * 2 + half, HT), :]

    def kb(fl, dx):
        return ((yl + fl) % 2) * 4 + (x + dx) % 4

    def htb(rows, fl, dx):
        return ht.at[rows, at(kb(fl, dx), TB)]

    def hth(rows, core_of):
        return ht.at[rows, at(kb(0, 0) * 2 + core_of, HT)]

    def pt(fl, dx, rows):
        return part.at[kb(fl, dx), rows, :]

    def ptc(fl, dx, rows, core_of):
        return part.at[kb(fl, dx), rows, at(core_of, HT)]

    def same(name, ref, to):
        return remote(name, ref, ref, to)

    half_q, half_o = at(q, FH), at(o, FH)

    D = {
        "HS": remote("HS", hs, hth(pl.ds(0, FH), q), core),
        "D1": remote("D1", dy_ref, dyb(q, 0, 0), core),
        "D2": remote("D2", dy_ref, dyb(q, 0, 0), yhp),
        "D3": remote("D3", dy_ref, dyb(q, 0, 0), zp),
        "D4": remote("D4", dy_ref, dyb(q, 0, 0), zm),
        "W": remote("W", w_ref.at[half_o, :], wv.at[q], core),
        "D5a": same("D5a", dyh(3, 0, 0), zp),
        "D5b": same("D5b", dyh(1, 0, 1), zm),
        "D6": same("D6", dyb(q, 0, 1), zp),
        "D7": same("D7", dyb(q, 0, 1), zm),
        "D8a": same("D8a", dyh(3, 1, 0), zp),
        "D8b": same("D8b", dyh(1, 1, 1), zm),
        "HB1a": same("HB1a", hth(GB_, q), xp),
        "HB1b": same("HB1b", hth(GB_, o), xp),
        "HB2a": same("HB2a", hth(GB_, q), xm),
        "HB2b": same("HB2b", hth(GB_, o), xm),
        "HA1": same("HA1", htb(GA_, 0, 0), xp),
        "HA2": same("HA2", htb(GA_, 0, 0), xm),
        "HYA": same("HYA", htb(GA_, 0, 0), ylp),
        "HYB": same("HYB", htb(GB_, 0, 0), ylp),
        "HB3": same("HB3", htb(GB0, 0, 3), xp),
        "HB4": same("HB4", htb(GB1, 0, 1), xm),
        "HYB2": same("HYB2", htb(GB_, 0, 3), ylp),
        "HYB3": same("HYB3", htb(GB_, 0, 1), ylp),
        "HYB4": same("HYB4", htb(GB0, 0, 2), ylp),
        "HYB5": same("HYB5", htb(GB1, 0, 2), ylp),
        "HA3a": same("HA3a", htb(GA0, 1, 0), xp),
        "HA3b": same("HA3b", htb(GA1, 1, 0), xp),
        "HA4a": same("HA4a", htb(GA0, 1, 0), xm),
        "HA4b": same("HA4b", htb(GA1, 1, 0), xm),
        "HA5a": same("HA5a", htb(GA0, 0, 3), xp),
        "HA5b": same("HA5b", htb(GA1, 0, 1), xm),
        "HA6a": same("HA6a", htb(GA0, 1, 3), xp),
        "HA6b": same("HA6b", htb(GA1, 1, 1), xm),
        "S1P": remote("S1P", pt(0, 2, A), r1p, xp),
        "S1M": remote("S1M", pt(1, 2, A), r1m, xm),
        "SB1P": remote("SB1P", pt(0, 2, B0), b1p, xp),
        "SB1M": remote("SB1M", pt(0, 2, B1), b1m, xm),
    }
    for i, r in enumerate((A0, A1)):
        D[f"S2PS{i}"] = remote(f"S2PS{i}", pt(1, 1, r), r2ps.at[r, :], xp)
        D[f"S2MS{i}"] = remote(f"S2MS{i}", pt(0, 3, r), r2ms.at[r, :], xm)
        D[f"S2PC{i}"] = remote(f"S2PC{i}", pt(0, 1, r), r2pc.at[r, :], xp)
        D[f"S2MC{i}"] = remote(f"S2MC{i}", pt(1, 3, r), r2mc.at[r, :], xm)
        for who, to, c in (("s", ylp, q), ("x", ylo, o)):
            D[f"SYA{i}{who}"] = remote(f"SYA{i}{who}", ptc(1, 0, r, c), ry.at[q, r, :], to)
    for dx in range(4):
        D[f"SYB{dx}"] = remote(f"SYB{dx}", pt(1, dx, B), by.at[(x + dx) % 4], ylp)
    for dz, fl in ((3, 0), (1, 0), (0, 1), (2, 0), (1, 1), (3, 1), (2, 1)):
        D[f"C{dz}{fl}"] = same(f"C{dz}{fl}", dyb(q, dz, fl), core)
    for m in range(2):
        D[f"GD{m}"] = remote(f"GD{m}", gdv.at[pl.ds(m * MT, MT), :],
                             gd_ref.at[pl.ds(pl.multiple_of(q * FH + m * MT, MT), MT), :], core)
    for who, up_to, down_to, c in (("s", xp, xm, q), ("x", xpo, xmo, o)):
        for n, dx, rows, dst, first, to in (("SB2Pi", 1, B1, b2p, HB, up_to), ("SB2Pd", 1, B0, b2p, 0, up_to),
                                            ("SB2Mi", 3, B0, b2m, 0, down_to), ("SB2Md", 3, B1, b2m, HB, down_to)):
            D[n + who] = remote(n + who, ptc(0, dx, rows, c), dst.at[q, pl.ds(first, HB), :], to)
    for n, rows in (("TA", A), ("TB", B)):
        D[n] = remote(n, tots.at[rows, :], tot.at[q, rows, :], core)

    def go(*names):
        for n in names:
            D[n].start()

    def got(*names):
        for n in names:
            D[n].wait_recv()

    local = {
        "g": pltpu.make_async_copy(gate_ref, gv, ls.at[0]),
        "u": pltpu.make_async_copy(up_ref, uv, ls.at[1]),
        "dy": pltpu.make_async_copy(dy_ref, dyb(q, 0, 0), ls.at[2]),
        "w": pltpu.make_async_copy(w_ref.at[half_q, :], wv.at[q], ls.at[3]),
    }

    bar = pltpu.get_barrier_semaphore()
    for to in (core, xp, xm, ylp, zp, zm, yhp, xpo, xmo, ylo):
        pl.semaphore_signal(bar, inc=1, device_id=to, device_id_type=MESH)
    for n in ("g", "u", "dy", "w"):
        local[n].start()

    def hidden(first, last, half, dst, lanes):
        def tile(i, _):
            s = at(i, 128)
            f = pl.ds(pl.multiple_of(half * FH + i * 128, 128), 128)
            gt, ut = gv[:, f].astype(F32), uv[:, f].astype(F32)
            h = gt * jax.nn.sigmoid(gt) * ut
            dst[s, lanes] = h.T.astype(BF)
            return 0

        lax.fori_loop(first, last, tile, 0)

    own = at(kb(0, 0) * 2 + q, HT)
    local["g"].wait()
    local["u"].wait()
    hidden(RA // 128, FH // 128, q, ht, own)
    pl.semaphore_wait(bar, 10)

    go("D2", "D3", "D4", "HB1a", "HB2a")
    hidden(0, FH // 128, o, hs, pl.ds(0, HT))
    go("HS")
    hidden(0, RA // 128, q, ht, own)
    go("D1", "W")
    got("HS")
    go("HYA", "HB1b", "HB2b", "HA1", "HA2", "HYB")

    def factors(i, _):
        f = at(i, 128)
        gt, ut = gv[:, f].astype(F32), uv[:, f].astype(F32)
        sig = jax.nn.sigmoid(gt)
        fg[:, f] = ut * sig * (1.0 + gt * (1.0 - sig))
        fu[:, f] = gt * sig
        return 0

    order = ((0, 0), (3, 0), (1, 0), (0, 1), (3, 1), (1, 1), (2, 0), (2, 1))

    def serve1(s):
        if s == 0:
            got("HB1a", "HB2a", "HB1b", "HB2b")
            go("HB3", "HB4", "HYB2", "HYB3")
            got("D3", "D4", "D2")
            go("D6", "D7", "D5a", "D5b", "C30", "C10", "C01")
            local["dy"].wait()
            local["w"].wait()
            got("W", "D1")
        elif s == 1:
            got("C30")
        elif s == 2:
            got("C10")
        elif s == 3:
            got("HA1", "HA2")
            go("HA5a", "HA5b")
            got("HYA")
            go("HA3a", "HA4b", "HA3b", "HA4a")
            got("C01")
        elif s == 4:
            got("HB3", "HB4")
            go("HYB4", "HYB5")
            got("D6", "D7")
            go("D8a", "D8b", "C31", "C11")
            got("C31")
        elif s == 5:
            got("C11")
        elif s == 6:
            got("D5a", "D5b")
            go("C20")
            got("C20")
        elif s == 7:
            got("HA3a", "HA4b")
            go("HA6a", "HA6b")
            got("D8a", "D8b")
            go("C21")
            got("C21")

    def step1(s, _):
        for i in range(8):
            pl.when(s == i)(functools.partial(serve1, i))
        dz = fl = jnp.int32(0)
        for i, (a, b) in enumerate(order):
            dz = jnp.where(s == i, a, dz)
            fl = jnp.where(s == i, b, fl)
        c = cb(dz, fl)

        def tile(m, _):
            rows = at(m, MT)
            acc = None
            for p in range(2):
                d = lax.dot_general(wv[p, rows, :], dyv[p, at(c, TB), :], NT, preferred_element_type=F32)
                acc = d if acc is None else acc + d
            part[c, rows, :] = acc.astype(BF)
            return 0

        lax.fori_loop(0, FH // MT, tile, 0)
        return 0

    lax.fori_loop(0, 8, step1, 0)

    go("S1P", "S1M", "S2PS0", "S2MS0", "SYB2", "SYB1", "SYB3")

    def add(k, start, size, *others):
        def chunk(i, _):
            here = pl.ds(pl.multiple_of(start + i * 64, 64), 64)
            t = part[k, here, :].astype(F32)
            for ref, off in others:
                t = t + ref[pl.ds(pl.multiple_of(off + i * 64, 64), 64), :].astype(F32)
            part[k, here, :] = t.astype(BF)
            return 0

        lax.fori_loop(0, size // 64, chunk, 0)

    def serve2(s):
        if s == 0:
            lax.fori_loop(0, 2 * FH // 128, factors, 0)
            got("HYB", "HYB2", "HYB3", "HYB4", "HYB5", "HA3b", "HA4a", "HA5a", "HA5b", "HA6a", "HA6b")
        elif s == 6:
            got("S1P", "S1M")
            add(kb(0, 1), 0, HA, (r1p, 0))
            add(kb(1, 3), 0, HA, (r1m, 0))
            go("S2PC0", "S2MC0", "S2PS1", "S2MS1")
            add(kb(0, 1), HA, HA, (r1p, HA))
            add(kb(1, 3), HA, HA, (r1m, HA))
            go("S2PC1", "S2MC1")
            got("SYB2")
            add(kb(0, 2), RA, RB, (by.at[(x + 2) % 4], 0))
            go("SB1P", "SB1M")
        elif s == 13:
            got("S2PS0", "S2MC0")
            add(kb(1, 0), 0, HA, (r2ps, 0), (r2mc, 0))
            go("SYA0s", "SYA0x", "SYB0", "GD0", "GD1")
            got("SYB1", "SYB3")
            add(kb(0, 1), RA, RB, (by.at[(x + 1) % 4], 0))
            add(kb(0, 3), RA, RB, (by.at[(x + 3) % 4], 0))
            go("SB2Pis", "SB2Mis", "SB2Pix", "SB2Mix")

    def step2(s, _):
        for i in (0, 6, 13):
            pl.when(s == i)(functools.partial(serve2, i))
        m = (s // 4) % 2
        rows, cols = at(m, MT), at(s % 4, NTILE)

        def tile(p):
            return lax.dot_general(ht[rows, :], dyv[p, :, cols], NN, preferred_element_type=F32).astype(BF)

        t = tile(jnp.where(s < 8, o, q))

        @pl.when(s < 8)
        def _():
            gdv[rows, cols] = t

        @pl.when(s >= 8)
        def _():
            gd_ref[pl.ds(pl.multiple_of(q * FH + m * MT, MT), MT), cols] = t

        return 0

    lax.fori_loop(0, 16, step2, 0)

    got("S2PS1", "S2MC1")
    add(kb(1, 0), HA, HA, (r2ps, HA), (r2mc, HA))
    go("SYA1s", "SYA1x")
    got("SB1P", "SB1M")
    add(kb(0, 1), RA, HB, (b1p, 0))
    add(kb(0, 3), RA + HB, HB, (b1m, 0))
    go("SB2Pds", "SB2Mds", "SB2Pdx", "SB2Mdx")

    def total(start, size, *others):
        def chunk(i, _):
            here = pl.ds(pl.multiple_of(start + i * 64, 64), 64)
            off = at(i, 64)
            for c, dst in ((q, tot.at[q]), (o, tots)):
                lanes = at(c, HT)
                t = part[kb(0, 0), here, lanes].astype(F32)
                for ref in others:
                    t = t + ref[off, lanes].astype(F32)
                dst[here, :] = t
            return 0

        lax.fori_loop(0, size // 64, chunk, 0)

    got("S2PC0", "S2MS0", "S2PC1", "S2MS1")
    total(0, RA, r2pc, r2ms)
    go("TA")
    got("SYB0")
    total(RA, RB, by.at[x])
    go("TB")

    got("GD0", "GD1", "TA", "TB", "SYA0s", "SYA0x", "SYA1s", "SYA1x")
    for n in D:
        if n.startswith("SB2"):
            D[n].wait_recv()
    for n in D:
        D[n].wait_send()


def finish(gd, tot, ry, b2p, b2m, fg, fu, gg_ref, gu_ref, gd_ref, og, ou, sems):
    cs = []

    def put(src, dst):
        c = pltpu.make_async_copy(src, dst, sems.at[len(cs)])
        c.start()
        cs.append(c)

    for i in range(8):
        rows = pl.ds(i * (FH // 4), FH // 4)
        put(gd.at[rows, :], gd_ref.at[rows, :])
    for h in range(2):
        def tile(first, *others):
            def body(i, _):
                s = at(i, 128)
                f = pl.ds(pl.multiple_of(h * FH + i * 128, 128), 128)
                t = tot[h, s, :]
                for ref in others:
                    t = t + ref[h, at(i - first, 128), :].astype(F32)
                gh = t.T
                og[:, f] = (gh * fg[:, f]).astype(BF)
                ou[:, f] = (gh * fu[:, f]).astype(BF)
                return 0

            return body

        lax.fori_loop(0, RA // 128, tile(0, ry), 0, unroll=True)
        lax.fori_loop(RA // 128, FH // 128, tile(RA // 128, b2p, b2m), 0, unroll=True)
        cols = pl.ds(h * FH, FH)
        put(og.at[:, cols], gg_ref.at[:, cols])
        put(ou.at[:, cols], gu_ref.at[:, cols])
    for c in cs:
        c.wait()


def local(grad_out, gate_act, up_act, down_weight):
    hbm = pl.BlockSpec(memory_space=pltpu.HBM)
    vmem = pl.BlockSpec(memory_space=pltpu.VMEM)
    block = lambda *s: pltpu.VMEM(s, BF)
    wide = lambda *s: pltpu.VMEM(s, F32)
    tokens, weight = gate_act.shape, down_weight.shape
    held = pl.pallas_call(
        kernel,
        out_shape=(
            block(*weight), wide(2, FH, HT), block(2, RA, HT), block(2, RB, HT), block(2, RB, HT),
            wide(*tokens), wide(*tokens),
        ),
        in_specs=[hbm] * 4,
        out_specs=(vmem,) * 7,
        scratch_shapes=[
            block(2, FH, DB), block(2, 8 * TB, DB), block(FH, 8 * TB), block(FH, HT),
            block(HT, 2 * FH), block(HT, 2 * FH),
            block(8, FH, TB),
            block(RA, TB), block(RA, TB), block(RA, TB), block(RA, TB), block(RA, TB), block(RA, TB),
            block(4, RB, TB), block(HB, TB), block(HB, TB),
            block(FH, DB), wide(FH, HT),
            pltpu.SemaphoreType.DMA((90,)), pltpu.SemaphoreType.DMA((90,)), pltpu.SemaphoreType.DMA((4,)),
        ],
        compiler_params=pltpu.CompilerParams(
            collective_id=0, has_side_effects=True, vmem_limit_bytes=46 * 2**20
        ),
        name="swiglu_down_backward",
    )(grad_out, gate_act, up_act, down_weight)
    return pl.pallas_call(
        finish,
        out_shape=tuple(jax.ShapeDtypeStruct(s, BF) for s in (tokens, tokens, weight)),
        in_specs=[vmem] * 7,
        out_specs=(hbm,) * 3,
        scratch_shapes=[block(*tokens), block(*tokens), pltpu.SemaphoreType.DMA((12,))],
        compiler_params=pltpu.CompilerParams(vmem_limit_bytes=6 * 2**20),
        name="finish",
    )(*held)


def solution(mesh):
    return jax.shard_map(
        local,
        mesh=mesh,
        in_specs=(P("col", "row"), P("row", "col"), P("row", "col"), P("col", "row")),
        out_specs=(P("row", "col"), P("row", "col"), P("col", "row")),
        check_vma=False,
    )
```
